32 devices in a mesh: row: 2 (over x), col: 4 (over z), depth: 4 (over y, core).
Axes of the slice: x: 2, y: 2, z: 4, core: 2. Of those that a mesh axis runs over, the one named last changes fastest.
Arguments:
- inputs: bfloat16 [128, 5120], P(('row', 'depth'), 'col'), may hold values from -6 to 6
- targets: bfloat16 [128, 5120], P(('row', 'depth'), 'col'), may hold values from -6 to 6
- norm_gain: float32 [5120], P('col'), may hold values from 0.5 to 1.5
- w_gate: bfloat16 [5120, 8192], P('col', ('row', 'depth')), may hold values from -0.078125 to 0.078125
- w_up: bfloat16 [5120, 8192], P('col', ('row', 'depth')), may hold values from -0.078125 to 0.078125
- w_down: bfloat16 [8192, 5120], P(('row', 'depth'), 'col'), may hold values from -0.0625 to 0.0625
- probe_gate: bfloat16 [5120, 8192], P('col', ('row', 'depth')), may hold values from -1 to 1, as said below
- probe_up: bfloat16 [5120, 8192], P('col', ('row', 'depth')), may hold values from -1 to 1, as said below
- probe_down: bfloat16 [8192, 5120], P(('row', 'depth'), 'col'), may hold values from -1 to 1, as said below
- moment_gate: float32 [5120, 8192], P('col', ('row', 'depth')), may hold values from -18 to 18
- moment_up: float32 [5120, 8192], P('col', ('row', 'depth')), may hold values from -18 to 18
- moment_down: float32 [8192, 5120], P(('row', 'depth'), 'col'), may hold values from -18 to 18
- second_gate: float32 [5120, 8192], P('col', ('row', 'depth')), may hold values from 1 to 100
- second_up: float32 [5120, 8192], P('col', ('row', 'depth')), may hold values from 1 to 100
- second_down: float32 [8192, 5120], P(('row', 'depth'), 'col'), may hold values from 1 to 100
Outputs:
- new_moment_gate: float32 [5120, 8192], P('col', ('row', 'depth'))
- new_moment_up: float32 [5120, 8192], P('col', ('row', 'depth'))
- new_moment_down: float32 [8192, 5120], P(('row', 'depth'), 'col')
- new_second_gate: float32 [5120, 8192], P('col', ('row', 'depth'))
- new_second_up: float32 [5120, 8192], P('col', ('row', 'depth'))
- new_second_down: float32 [8192, 5120], P(('row', 'depth'), 'col')
- step_gate: float32 [5120, 8192], P('col', ('row', 'depth'))
- step_up: float32 [5120, 8192], P('col', ('row', 'depth'))
- step_down: float32 [8192, 5120], P(('row', 'depth'), 'col')
The draws below stay inside these ranges and needn't reach their ends.
Inputs may be any that keep to these rules, and one draw needn't show every extreme that they name: `probe_gate`: every entry is +1 or -1. `probe_up`: every entry is +1 or -1. `probe_down`: every entry is +1 or -1.
All inputs are finite; a program needn't handle non-finite values.
Results may differ from the reference program's by a relative error of at most 0.0046.
Values may be sent and summed in bfloat16 or wider, within the bound.
A program may use at most 192 MiB of HBM per device.

```python
import math
import jax
import jax.numpy as jnp
from jax import lax

D = 5120
FF = 8192
TILE = 128
STEP = 1000
TOKENS = 128


def rademacher(key, height, breadth):
    coins = jax.random.randint(key, (height, breadth), 0, 2)
    return (2.0 * coins.astype(jnp.float32) - 1.0).astype(jnp.bfloat16)


def draw_probe_gate(key, part):
    return rademacher(jax.random.fold_in(key, 101), D, FF)


def draw_probe_up(key, part):
    return rademacher(jax.random.fold_in(key, 202), D, FF)


def draw_probe_down(key, part):
    return rademacher(jax.random.fold_in(key, 303), FF, D)


def shard_levels(key, extent, cuts, low, high):
    factor_of = 1.0
    for axis_at, parts in cuts:
        heights = jax.random.uniform(jax.random.fold_in(jax.random.fold_in(key, 6), axis_at), (parts,), jnp.float32, low / len(cuts), high / len(cuts))
        factor_of = factor_of * jnp.repeat(jnp.exp(heights), extent[axis_at] // parts).reshape((-1,) + (1,) * (len(extent) - 1 - axis_at))
    return factor_of


def gaussian(key, extent, spread, reach, pieces=(), kind=jnp.bfloat16):
    loudness = shard_levels(key, extent, pieces, -0.22, 0.18) if pieces else 1.0
    array = jax.random.normal(key, extent, jnp.float32) * spread * loudness
    return jnp.minimum(jnp.maximum(array, -reach), reach).astype(kind)


def setup_inputs(seed: int = 0) -> dict:
    seeds = jax.random.split(jax.random.key(seed), 16)
    inputs = gaussian(seeds[0], (TOKENS, D), 1.0, 6.0, ((0, 8), (1, 4)))
    targets = gaussian(seeds[1], (TOKENS, D), 1.0, 6.0, ((0, 8), (1, 4)))
    norm_gain = jnp.clip(1.0 + 0.1 * jax.random.normal(seeds[2], (D,), jnp.float32), 0.5, 1.5)
    w_gate = gaussian(seeds[3], (D, FF), D ** -0.5, 0.078125, ((0, 4), (1, 8)))
    w_up = gaussian(seeds[4], (D, FF), D ** -0.5, 0.078125, ((0, 4), (1, 8)))
    w_down = gaussian(seeds[5], (FF, D), FF ** -0.5, 0.0625, ((0, 8), (1, 4)))
    probe_gate = draw_probe_gate(jax.random.fold_in(seeds[15], 71), 0)
    probe_up = draw_probe_up(jax.random.fold_in(seeds[15], 71), 0)
    probe_down = draw_probe_down(jax.random.fold_in(seeds[15], 71), 0)
    moment_gate = gaussian(seeds[9], (D, FF), 3.0, 18.0, ((0, 4), (1, 8)), jnp.float32)
    moment_up = gaussian(seeds[10], (D, FF), 3.0, 18.0, ((0, 4), (1, 8)), jnp.float32)
    moment_down = gaussian(seeds[11], (FF, D), 3.0, 18.0, ((0, 8), (1, 4)), jnp.float32)
    second_gate = jnp.clip(jnp.exp(math.log(100.0) - 4.6051702 * jax.random.uniform(seeds[12], (D, FF), jnp.float32) ** shard_levels(seeds[12], (D, FF), ((0, 4), (1, 8)), -0.2, 0.2)), 1.0, 100.0)
    second_up = jnp.clip(jnp.exp(math.log(100.0) - 4.6051702 * jax.random.uniform(seeds[13], (D, FF), jnp.float32) ** shard_levels(seeds[13], (D, FF), ((0, 4), (1, 8)), -0.2, 0.2)), 1.0, 100.0)
    second_down = jnp.clip(jnp.exp(math.log(100.0) - 4.6051702 * jax.random.uniform(seeds[14], (FF, D), jnp.float32) ** shard_levels(seeds[14], (FF, D), ((0, 8), (1, 4)), -0.2, 0.2)), 1.0, 100.0)
    return {"inputs": inputs, "targets": targets, "norm_gain": norm_gain, "w_gate": w_gate, "w_up": w_up, "w_down": w_down, "probe_gate": probe_gate, "probe_up": probe_up, "probe_down": probe_down, "moment_gate": moment_gate, "moment_up": moment_up, "moment_down": moment_down, "second_gate": second_gate, "second_up": second_up, "second_down": second_down}


beta_one = 0.9
beta_two = 0.999
adam_floor = 1e-08
norm_floor = 1e-05

def silu_parts(gate_pre):
    sig = jax.nn.sigmoid(gate_pre)
    act = gate_pre * sig
    slope = sig * (1.0 + gate_pre * (1.0 - sig))
    bend = sig * (1.0 - sig) * (2.0 + gate_pre * (1.0 - 2.0 * sig))
    return (act, slope, bend)

def tile_means(product):
    height, breadth = product.shape
    blocks = product.reshape(height // TILE, TILE, breadth // TILE, TILE)
    means = lax.optimization_barrier(jnp.mean(blocks, axis=(1, 3), keepdims=True))
    return jnp.broadcast_to(means, blocks.shape).reshape(height, breadth)

def adahessian(moment, second, gradient, curvature, probe):
    averaged = tile_means(probe.astype(jnp.float32) * curvature)
    new_moment = beta_one * moment + (1.0 - beta_one) * gradient
    new_second = beta_two * second + (1.0 - beta_two) * averaged * averaged
    corrected = new_moment / (1.0 - beta_one ** STEP)
    scale_root = jnp.sqrt(new_second / (1.0 - beta_two ** STEP))
    return (new_moment, new_second, corrected / (scale_root + adam_floor))

def matmul(left, right):
    return jnp.dot(left, right, preferred_element_type=jnp.float32)

def inner_left(left, right):
    return lax.dot_general(left, right, (((0,), (0,)), ((), ())), preferred_element_type=jnp.float32)

def inner_right(left, right):
    return lax.dot_general(left, right, (((1,), (1,)), ((), ())), preferred_element_type=jnp.float32)

def reference(inputs, targets, norm_gain, w_gate, w_up, w_down, probe_gate, probe_up, probe_down, moment_gate, moment_up, moment_down, second_gate, second_up, second_down):
    feats = inputs.astype(jnp.float32)
    meansq = lax.optimization_barrier(jnp.mean(feats * feats, axis=1, keepdims=True))
    normed = (feats * lax.rsqrt(meansq + norm_floor) * norm_gain).astype(jnp.bfloat16)
    gate_pre = matmul(normed, w_gate)
    up_pre = matmul(normed, w_up)
    gate_tan = matmul(normed, probe_gate)
    up_tan = matmul(normed, probe_up)
    act, slope, bend = silu_parts(gate_pre)
    hidden = (act * up_pre).astype(jnp.bfloat16)
    hidden_tan = (slope * gate_tan * up_pre + act * up_tan).astype(jnp.bfloat16)
    outputs = feats + matmul(hidden, w_down)
    error = (outputs - targets.astype(jnp.float32)).astype(jnp.bfloat16)
    error_tan = (matmul(hidden_tan, w_down) + matmul(hidden, probe_down)).astype(jnp.bfloat16)
    back_hidden = inner_right(error, w_down)
    back_tan = inner_right(error_tan, w_down) + inner_right(error, probe_down)
    back_gate = (back_hidden * up_pre * slope).astype(jnp.bfloat16)
    back_up = (back_hidden * act).astype(jnp.bfloat16)
    gate_tan_back = (back_tan * up_pre * slope + back_hidden * up_tan * slope + back_hidden * up_pre * bend * gate_tan).astype(jnp.bfloat16)
    up_tan_back = (back_tan * act + back_hidden * slope * gate_tan).astype(jnp.bfloat16)
    grad_gate = inner_left(normed, back_gate)
    grad_up = inner_left(normed, back_up)
    grad_down = inner_left(hidden, error)
    curve_gate = inner_left(normed, gate_tan_back)
    curve_up = inner_left(normed, up_tan_back)
    curve_down = inner_left(hidden_tan, error) + inner_left(hidden, error_tan)
    gate_moment, gate_second, gate_step = adahessian(moment_gate, second_gate, grad_gate, curve_gate, probe_gate)
    up_moment, up_second, up_step = adahessian(moment_up, second_up, grad_up, curve_up, probe_up)
    down_moment, down_second, down_step = adahessian(moment_down, second_down, grad_down, curve_down, probe_down)
    return (gate_moment, up_moment, down_moment, gate_second, up_second, down_second, gate_step, up_step, down_step)
```

```python
import functools

import jax
import jax.numpy as jnp
from jax import lax
from jax.experimental import pallas as pl
from jax.experimental.pallas import tpu as pltpu
from jax.sharding import PartitionSpec as P

TILE = 128
STEP = 1000

beta_one = 0.9
beta_two = 0.999
adam_floor = 1e-08
norm_floor = 1e-05

F32 = jnp.float32
BF16 = jnp.bfloat16
MESH = pl.DeviceIdType.MESH


def dot(left, right, dims):
    return lax.dot_general(left, right, ((dims[:1], dims[1:]), ((), ())), preferred_element_type=F32)


def exchange(
    n_row, n_col, n_depth,
    x_ref, t_ref, gain_ref, w_gate, w_up, w_down, p_gate, p_up, p_down,
    normed_ref, hid_ref, err_ref, back_ref,
    front, down, x_all, xg, sq_send, sq_recv, scale_all,
    part, part_in, coef, out_part, out_in, bk_part, bk_in,
    load_sem, x_s, x_r, sq_s, sq_r, sc_s, sc_r, part_s, part_r, hid_s, hid_r,
    out_s, out_r, err_s, err_r, bk_s, bk_r, back_s, back_r,
):
    n_group = n_row * n_depth
    row, c, depth = lax.axis_index("row"), lax.axis_index("col"), lax.axis_index("depth")
    g = row * n_depth + depth
    tokens, width = normed_ref.shape
    features = width * n_col
    hidden = w_gate.shape[1]
    tile_f, tile_d = min(256, hidden), min(256, width)

    loads = [
        pltpu.make_async_copy(src, dst, load_sem.at[i])
        for i, (src, dst) in enumerate([
            (w_gate, front.at[0]), (w_up, front.at[1]), (p_gate, front.at[2]), (p_up, front.at[3]),
            (w_down, down.at[0]), (p_down, down.at[1]),
        ])
    ]
    for load in loads:
        load.start()

    def group_id(k):
        to = lax.rem(g + k, n_group)
        return to, {"row": lax.div(to, n_depth), "depth": lax.rem(to, n_depth)}

    def col_id(k):
        to = lax.rem(c + k, n_col)
        return to, {"col": to}

    def remote(src, dst, send, recv, where):
        return pltpu.make_async_remote_copy(
            src_ref=src, dst_ref=dst, send_sem=send, recv_sem=recv, device_id=where, device_id_type=MESH
        )

    def group_loop(body):
        lax.fori_loop(1, n_group, lambda k, carry: (body(k), carry)[1], 0)

    barrier = pltpu.get_barrier_semaphore()

    def greet(k):
        pl.semaphore_signal(barrier, inc=1, device_id=group_id(k)[1], device_id_type=MESH)

    group_loop(greet)
    for k in range(1, n_col):
        pl.semaphore_signal(barrier, inc=1, device_id=col_id(k)[1], device_id_type=MESH)
    pl.semaphore_wait(barrier, n_group + n_col - 2)

    def x_copy(k):
        return remote(x_ref, x_all.at[g], x_s.at[k], x_r.at[k], group_id(k)[1])

    def sq_copy(k):
        to, where = col_id(k)
        return remote(sq_send.at[to], sq_recv.at[c], sq_s.at[k], sq_r.at[k], where)

    def sc_copy(k):
        return remote(scale_all.at[c], scale_all.at[c], sc_s.at[k], sc_r.at[k], col_id(k)[1])

    def part_copy(a, k):
        to, where = col_id(k)
        return remote(part.at[a, to], part_in.at[a, c], part_s.at[a, k], part_r.at[a, k], where)

    def hid_copy(a, k):
        return remote(hid_ref.at[a, c], hid_ref.at[a, c], hid_s.at[a, k], hid_r.at[a, k], col_id(k)[1])

    def out_copy(a, k):
        to, where = group_id(k)
        return remote(out_part.at[a, to], out_in.at[a, g], out_s.at[a, k], out_r.at[a, k], where)

    def err_copy(a, k):
        return remote(err_ref.at[a, g], err_ref.at[a, g], err_s.at[a, k], err_r.at[a, k], group_id(k)[1])

    def bk_copy(a, k):
        to, where = col_id(k)
        return remote(bk_part.at[a, to], bk_in.at[a, c], bk_s.at[a, k], bk_r.at[a, k], where)

    def back_copy(a, k):
        return remote(back_ref.at[a, c], back_ref.at[a, c], back_s.at[a, k], back_r.at[a, k], col_id(k)[1])

    def col_each(act, *at):
        for k in range(1, n_col):
            act(*at, k)

    group_loop(lambda k: x_copy(k).start())
    x_all[g] = x_ref[...]
    group_loop(lambda k: x_copy(k).wait_recv())
    feats = x_all[...].reshape(tokens, width).astype(F32)
    squares = jnp.sum(feats * feats, axis=1, keepdims=True)
    sq_send[...] = jnp.broadcast_to(squares, (tokens, 128)).reshape(sq_send.shape)
    col_each(lambda k: sq_copy(k).start())
    xg[...] = (feats * gain_ref[...]).astype(BF16)

    for a in range(4):
        loads[a].wait()

        @pl.loop(0, hidden // tile_f)
        def _(j):
            cols = pl.ds(pl.multiple_of(j * tile_f, tile_f), tile_f)
            value = dot(xg[...], front[a, :, cols], (1, 0))
            part[a, :, :, cols] = value.astype(BF16).reshape(n_col, tokens // n_col, tile_f)

        col_each(lambda a, k: part_copy(a, k).start(), a)

    total = sq_send[c]
    for k in range(1, n_col):
        sq_copy(k).wait_recv()
        total = total + sq_recv[lax.rem(c - k + n_col, n_col)]
    scale = lax.rsqrt(total / features + norm_floor)
    scale_all[c] = scale
    col_each(lambda k: sc_copy(k).start())

    def summed(own, came, copy, a):
        value = own[a, c].astype(F32)
        for k in range(1, n_col):
            copy(a, k).wait_recv()
            value = value + came[a, lax.rem(c - k + n_col, n_col)].astype(F32)
        return value

    scale = scale[:, :1]
    gate_pre = summed(part, part_in, part_copy, 0) * scale
    sig = jax.nn.sigmoid(gate_pre)
    act = gate_pre * sig
    slope = sig * (1.0 + gate_pre * (1.0 - sig))
    bend = sig * (1.0 - sig) * (2.0 + gate_pre * (1.0 - 2.0 * sig))
    coef[0] = act
    coef[1] = slope
    coef[2] = bend
    up_pre = summed(part, part_in, part_copy, 1) * scale
    hid_ref[0, c] = (coef[0] * up_pre).astype(BF16)
    col_each(lambda a, k: hid_copy(a, k).start(), 0)
    coef[3] = up_pre
    gate_tan = summed(part, part_in, part_copy, 2) * scale
    coef[4] = gate_tan
    up_tan = summed(part, part_in, part_copy, 3) * scale
    hid_ref[1, c] = (coef[1] * coef[4] * coef[3] + coef[0] * up_tan).astype(BF16)
    col_each(lambda a, k: hid_copy(a, k).start(), 1)
    coef[2] = up_tan * coef[1] + coef[3] * coef[2] * coef[4]
    coef[4] = coef[1] * coef[4]
    coef[1] = coef[3] * coef[1]

    def down_product(a, make):
        @pl.loop(0, width // tile_d)
        def _(j):
            cols = pl.ds(pl.multiple_of(j * tile_d, tile_d), tile_d)
            out_part[a, :, :, cols] = make(cols).astype(BF16).reshape(n_group, tokens // n_group, tile_d)

        group_loop(lambda k: out_copy(a, k).start())

    def flat(ref, a):
        value = ref[a]
        return value.reshape(tokens, value.shape[-1])

    loads[4].wait()
    loads[5].wait()
    col_each(lambda a, k: hid_copy(a, k).wait_recv(), 0)
    down_product(0, lambda cols: dot(flat(hid_ref, 0), down[0, :, cols], (1, 0)))
    col_each(lambda a, k: hid_copy(a, k).wait_recv(), 1)
    down_product(
        1,
        lambda cols: dot(flat(hid_ref, 1), down[0, :, cols], (1, 0))
        + dot(flat(hid_ref, 0), down[1, :, cols], (1, 0)),
    )

    def owner_sum(a, start):
        def add(k, value):
            out_copy(a, k).wait_recv()
            return value + out_in[a, lax.rem(g - k + n_group, n_group)].astype(F32)

        return lax.fori_loop(1, n_group, add, start + out_part[a, g].astype(F32))

    outputs = owner_sum(0, x_ref[...].astype(F32))
    err_ref[0, g] = (outputs - t_ref[...].astype(F32)).astype(BF16)
    group_loop(lambda k: err_copy(0, k).start())
    err_ref[1, g] = owner_sum(1, jnp.zeros(x_ref.shape, F32)).astype(BF16)
    group_loop(lambda k: err_copy(1, k).start())

    col_each(lambda k: sc_copy(k).wait_recv())
    scales = scale_all[...].reshape(tokens, 128)[:, :1]
    feats = x_all[...].reshape(tokens, width).astype(F32)
    normed_ref[...] = (feats * scales * gain_ref[...]).astype(BF16)

    def back_product(a, make):
        @pl.loop(0, hidden // tile_f)
        def _(j):
            rows = pl.ds(pl.multiple_of(j * tile_f, tile_f), tile_f)
            bk_part[a, :, :, rows] = make(rows).astype(BF16).reshape(n_col, tokens // n_col, tile_f)

        col_each(lambda a, k: bk_copy(a, k).start(), a)

    group_loop(lambda k: err_copy(0, k).wait_recv())
    back_product(0, lambda rows: dot(flat(err_ref, 0), down[0, rows, :], (1, 1)))
    group_loop(lambda k: err_copy(1, k).wait_recv())
    back_product(
        1,
        lambda rows: dot(flat(err_ref, 1), down[0, rows, :], (1, 1))
        + dot(flat(err_ref, 0), down[1, rows, :], (1, 1)),
    )

    back_hidden = summed(bk_part, bk_in, bk_copy, 0)
    back_ref[0, c] = (back_hidden * coef[1]).astype(BF16)
    col_each(lambda a, k: back_copy(a, k).start(), 0)
    back_ref[1, c] = (back_hidden * coef[0]).astype(BF16)
    col_each(lambda a, k: back_copy(a, k).start(), 1)
    back_tan = summed(bk_part, bk_in, bk_copy, 1)
    back_ref[2, c] = (back_tan * coef[1] + back_hidden * coef[2]).astype(BF16)
    col_each(lambda a, k: back_copy(a, k).start(), 2)
    back_ref[3, c] = (back_tan * coef[0] + back_hidden * coef[4]).astype(BF16)
    col_each(lambda a, k: back_copy(a, k).start(), 3)

    for a in range(4):
        col_each(lambda a, k: back_copy(a, k).wait_recv(), a)

    def sent(k):
        x_copy(k).wait_send()
        for a in range(2):
            out_copy(a, k).wait_send()
            err_copy(a, k).wait_send()

    group_loop(sent)
    for k in range(1, n_col):
        sq_copy(k).wait_send()
        sc_copy(k).wait_send()
        for a in range(4):
            part_copy(a, k).wait_send()
            back_copy(a, k).wait_send()
        for a in range(2):
            hid_copy(a, k).wait_send()
            bk_copy(a, k).wait_send()


def run_exchange(mesh, x, t, gain, w_gate, w_up, w_down, p_gate, p_up, p_down):
    n_row, n_col, n_depth = mesh.shape["row"], mesh.shape["col"], mesh.shape["depth"]
    n_group = n_row * n_depth
    rows, width = x.shape
    hidden = w_gate.shape[1]
    tokens = rows * n_group
    run = tokens // n_col
    vmem = pl.BlockSpec(memory_space=pltpu.VMEM)
    hbm = pl.BlockSpec(memory_space=pl.ANY)
    sem = pltpu.SemaphoreType.DMA
    pair = lambda *shape: [sem(shape), sem(shape)]
    shape = jax.ShapeDtypeStruct
    return pl.pallas_call(
        functools.partial(exchange, n_row, n_col, n_depth),
        out_shape=(
            shape((tokens, width), BF16),
            shape((2, n_col, run, hidden), BF16),
            shape((2, n_group, rows, width), BF16),
            shape((4, n_col, run, hidden), BF16),
        ),
        in_specs=[vmem] * 3 + [hbm] * 6,
        out_specs=(vmem,) * 4,
        scratch_shapes=[
            pltpu.VMEM((4, width, hidden), BF16),
            pltpu.VMEM((2, hidden, width), BF16),
            pltpu.VMEM((n_group, rows, width), BF16),
            pltpu.VMEM((tokens, width), BF16),
            pltpu.VMEM((n_col, run, 128), F32),
            pltpu.VMEM((n_col, run, 128), F32),
            pltpu.VMEM((n_col, run, 128), F32),
            pltpu.VMEM((4, n_col, run, hidden), BF16),
            pltpu.VMEM((4, n_col, run, hidden), BF16),
            pltpu.VMEM((5, run, hidden), F32),
            pltpu.VMEM((2, n_group, rows, width), BF16),
            pltpu.VMEM((2, n_group, rows, width), BF16),
            pltpu.VMEM((2, n_col, run, hidden), BF16),
            pltpu.VMEM((2, n_col, run, hidden), BF16),
            sem((6,)),
            *pair(n_group), *pair(n_col), *pair(n_col), *pair(4, n_col), *pair(2, n_col),
            *pair(2, n_group), *pair(2, n_group), *pair(2, n_col), *pair(4, n_col),
        ],
        compiler_params=pltpu.CompilerParams(
            collective_id=0, has_side_effects=True, vmem_limit_bytes=56 * 2**20
        ),
    )(x, t, gain.reshape(1, width), w_gate, w_up, w_down, p_gate, p_up, p_down)


def update_tile(moment, second, probe, grad, curve, new_moment, new_second, step, cols):
    product = probe[:, cols].astype(F32) * curve
    average = jnp.sum(product) * (1.0 / (TILE * TILE))
    moved = beta_one * moment[:, cols] + (1.0 - beta_one) * grad
    square = beta_two * second[:, cols] + (1.0 - beta_two) * average * average
    new_moment[:, cols] = moved
    new_second[:, cols] = square
    root = jnp.sqrt(square * (1.0 / (1.0 - beta_two**STEP)))
    step[:, cols] = moved * (1.0 / (1.0 - beta_one**STEP)) / (root + adam_floor)


def update_front(normed, back, moment, second, probe, new_moment, new_second, step):
    tokens = normed.shape[0]
    left = normed[...].T
    breadth = moment.shape[1]
    for j in range(breadth // TILE):
        cols = slice(j * TILE, (j + 1) * TILE)
        grad = dot(left, back[0, 0, :, :, cols].reshape(tokens, TILE), (1, 0))
        curve = dot(left, back[1, 0, :, :, cols].reshape(tokens, TILE), (1, 0))
        update_tile(moment, second, probe, grad, curve, new_moment, new_second, step, cols)


def update_down(hid, err, moment, second, probe, new_moment, new_second, step):
    tokens = err.shape[1] * err.shape[2]
    primal = hid[0].reshape(tokens, TILE).T
    tangent = hid[1].reshape(tokens, TILE).T
    breadth = moment.shape[1]
    for j in range(breadth // TILE):
        cols = slice(j * TILE, (j + 1) * TILE)
        error = err[0, :, :, cols].reshape(tokens, TILE)
        error_tan = err[1, :, :, cols].reshape(tokens, TILE)
        grad = dot(primal, error, (1, 0))
        curve = dot(tangent, error, (1, 0)) + dot(primal, error_tan, (1, 0))
        update_tile(moment, second, probe, grad, curve, new_moment, new_second, step, cols)


def run_update(body, acts, act_specs, moment, second, probe):
    height, breadth = moment.shape
    block = pl.BlockSpec((TILE, breadth), lambda i: (i, 0))
    return pl.pallas_call(
        body,
        grid=(height // TILE,),
        out_shape=(jax.ShapeDtypeStruct(moment.shape, F32),) * 3,
        in_specs=[*act_specs, block, block, block],
        out_specs=(block,) * 3,
        compiler_params=pltpu.CompilerParams(
            dimension_semantics=("arbitrary",), vmem_limit_bytes=40 * 2**20
        ),
    )(*acts, moment, second, probe)


def shards(
    mesh, inputs, targets, norm_gain, w_gate, w_up, w_down, probe_gate, probe_up, probe_down,
    moment_gate, moment_up, moment_down, second_gate, second_up, second_down,
):
    normed, hid, err, back = run_exchange(
        mesh, inputs, targets, norm_gain, w_gate, w_up, w_down, probe_gate, probe_up, probe_down
    )
    tokens = normed.shape[0]
    _, n_col, run, hidden = back.shape
    pairs = back.reshape(2, 2, n_col, run, hidden)
    normed_spec = pl.BlockSpec((tokens, TILE), lambda i: (0, i))

    def back_spec(which):
        return pl.BlockSpec((2, 1, n_col, run, hidden), lambda i: (0, which, 0, 0, 0))

    gate = run_update(
        update_front, (normed, pairs), (normed_spec, back_spec(0)), moment_gate, second_gate, probe_gate
    )
    up = run_update(
        update_front, (normed, pairs), (normed_spec, back_spec(1)), moment_up, second_up, probe_up
    )
    down = run_update(
        update_down,
        (hid, err),
        (
            pl.BlockSpec((2, n_col, run, TILE), lambda i: (0, 0, 0, i)),
            pl.BlockSpec(err.shape, lambda i: (0, 0, 0, 0)),
        ),
        moment_down, second_down, probe_down,
    )
    return (gate[0], up[0], down[0], gate[1], up[1], down[1], gate[2], up[2], down[2])


def solution(mesh):
    group = ("row", "depth")
    rows, cols = P(group, "col"), P("col", group)
    return jax.shard_map(
        functools.partial(shards, mesh),
        mesh=mesh,
        in_specs=(rows, rows, P("col"), cols, cols, rows) + (cols, cols, rows) * 3,
        out_specs=(cols, cols, rows) * 3,
        check_vma=False,
    )
```

```python
import functools
import math

import jax
import jax.numpy as jnp
from jax import lax
from jax.experimental import pallas as pl
from jax.experimental.pallas import tpu as pltpu
from jax.sharding import PartitionSpec as P

TILE = 128
STEP = 1000

beta_one = 0.9
beta_two = 0.999
adam_floor = 1e-08
norm_floor = 1e-05

F32 = jnp.float32
BF16 = jnp.bfloat16
MESH = pl.DeviceIdType.MESH


def dot(left, right, dims):
    return lax.dot_general(left, right, ((dims[:1], dims[1:]), ((), ())), preferred_element_type=F32)


def update(moment, second, probe, grad, curve):
    product = jnp.sum(probe.astype(F32) * curve, axis=0, keepdims=True)
    parts = []
    for j in range(second.shape[1] // TILE):
        cols = slice(j * TILE, (j + 1) * TILE)
        average = jnp.sum(product[:, cols], axis=1, keepdims=True) * (1.0 / (TILE * TILE))
        parts.append(beta_two * second[:, cols] + (1.0 - beta_two) * average * average)
    square = jnp.concatenate(parts, axis=1) if len(parts) > 1 else parts[0]
    moved = beta_one * moment + (1.0 - beta_one) * grad
    scaled = square * (1.0 / (1.0 - beta_two**STEP))
    root = scaled * lax.rsqrt(scaled)
    return moved, square, moved * (1.0 / (1.0 - beta_one**STEP)) / (root + adam_floor)


def exchange(
    n_row, n_col, n_depth,
    x_ref, t_ref, gain_ref, w_gate, w_up, w_down, p_gate, p_up, p_down,
    m_gate, m_up, m_down, s_gate, s_up, s_down,
    normed_ref, back_ref, probes, moments, seconds, new_moment, new_second, step,
    hid_ref, err_ref, front, down, x_all, xg, sq_send, sq_recv, scale_all,
    part, part_in, coef, out_part, out_in, bk_part, bk_in,
    load_sem, state_sem, x_s, x_r, sq_s, sq_r, sc_s, sc_r, part_s, part_r, hid_s, hid_r,
    out_s, out_r, err_s, err_r, bk_s, bk_r, back_s, back_r,
):
    n_group = n_row * n_depth
    row, c, depth = lax.axis_index("row"), lax.axis_index("col"), lax.axis_index("depth")
    g = row * n_depth + depth
    width, tokens = normed_ref.shape
    features = width * n_col
    hidden = w_gate.shape[1]
    tile_f, tile_d = min(256, hidden), min(256, width)

    loads = [
        pltpu.make_async_copy(src, dst, load_sem.at[i])
        for i, (src, dst) in enumerate([
            (w_gate, front.at[0]), (w_up, front.at[1]), (p_gate, probes.at[0]), (p_up, probes.at[1]),
            (w_down, down.at[0]), (p_down, down.at[1]),
        ])
    ]
    states = [
        pltpu.make_async_copy(src, dst, state_sem.at[i])
        for i, (src, dst) in enumerate([
            (m_down, new_moment), (s_down, new_second), (m_gate, moments.at[0]), (s_gate, seconds.at[0]),
            (m_up, moments.at[1]), (s_up, seconds.at[1]),
        ])
    ]
    for load in loads:
        load.start()

    def group_id(k):
        to = lax.rem(g + k, n_group)
        return to, {"row": lax.div(to, n_depth), "depth": lax.rem(to, n_depth)}

    def col_id(k):
        to = lax.rem(c + k, n_col)
        return to, {"col": to}

    def remote(src, dst, send, recv, where):
        return pltpu.make_async_remote_copy(
            src_ref=src, dst_ref=dst, send_sem=send, recv_sem=recv, device_id=where, device_id_type=MESH
        )

    def group_loop(body):
        lax.fori_loop(1, n_group, lambda k, carry: (body(k), carry)[1], 0)

    barrier = pltpu.get_barrier_semaphore()

    def greet(k):
        pl.semaphore_signal(barrier, inc=1, device_id=group_id(k)[1], device_id_type=MESH)

    group_loop(greet)
    for k in range(1, n_col):
        pl.semaphore_signal(barrier, inc=1, device_id=col_id(k)[1], device_id_type=MESH)
    pl.semaphore_wait(barrier, n_group + n_col - 2)

    def x_copy(k):
        return remote(x_ref, x_all.at[g], x_s.at[k], x_r.at[k], group_id(k)[1])

    def sq_copy(k):
        to, where = col_id(k)
        return remote(sq_send.at[to], sq_recv.at[c], sq_s.at[k], sq_r.at[k], where)

    def sc_copy(k):
        return remote(scale_all.at[c], scale_all.at[c], sc_s.at[k], sc_r.at[k], col_id(k)[1])

    def part_copy(a, k):
        to, where = col_id(k)
        return remote(part.at[a, to], part_in.at[a, c], part_s.at[a, k], part_r.at[a, k], where)

    def hid_copy(a, k):
        return remote(hid_ref.at[a, c], hid_ref.at[a, c], hid_s.at[a, k], hid_r.at[a, k], col_id(k)[1])

    def out_copy(a, k):
        to, where = group_id(k)
        return remote(out_part.at[a, to], out_in.at[a, g], out_s.at[a, k], out_r.at[a, k], where)

    def err_copy(a, k):
        return remote(err_ref.at[a, g], err_ref.at[a, g], err_s.at[a, k], err_r.at[a, k], group_id(k)[1])

    def bk_copy(a, k):
        to, where = col_id(k)
        return remote(bk_part.at[a, to], bk_in.at[a, c], bk_s.at[a, k], bk_r.at[a, k], where)

    def back_copy(a, k):
        return remote(back_ref.at[a, c], back_ref.at[a, c], back_s.at[a, k], back_r.at[a, k], col_id(k)[1])

    def col_each(act, *at):
        for k in range(1, n_col):
            act(*at, k)

    group_loop(lambda k: x_copy(k).start())
    x_all[g] = x_ref[...]
    group_loop(lambda k: x_copy(k).wait_recv())
    feats = x_all[...].reshape(tokens, width).astype(F32)
    squares = jnp.sum(feats * feats, axis=1, keepdims=True)
    sq_send[...] = jnp.broadcast_to(squares, (tokens, 128)).reshape(sq_send.shape)
    col_each(lambda k: sq_copy(k).start())
    xg[...] = (feats * gain_ref[...]).astype(BF16)

    for a in range(4):
        loads[a].wait()

        @pl.loop(0, hidden // tile_f)
        def _(j):
            cols = pl.ds(pl.multiple_of(j * tile_f, tile_f), tile_f)
            weight = front[a, :, cols] if a < 2 else probes[a - 2, :, cols]
            value = dot(xg[...], weight, (1, 0))
            part[a, :, :, cols] = value.astype(BF16).reshape(n_col, tokens // n_col, tile_f)

        col_each(lambda a, k: part_copy(a, k).start(), a)

    for state in states:
        state.start()
    total = sq_send[c]
    for k in range(1, n_col):
        sq_copy(k).wait_recv()
        total = total + sq_recv[lax.rem(c - k + n_col, n_col)]
    scale = lax.rsqrt(total / features + norm_floor)
    scale_all[c] = scale
    col_each(lambda k: sc_copy(k).start())

    def summed(own, came, copy, a):
        value = own[a, c].astype(F32)
        for k in range(1, n_col):
            copy(a, k).wait_recv()
            value = value + came[a, lax.rem(c - k + n_col, n_col)].astype(F32)
        return value

    scale = scale[:, :1]
    gate_pre = summed(part, part_in, part_copy, 0) * scale
    sig = jax.nn.sigmoid(gate_pre)
    act = gate_pre * sig
    slope = sig * (1.0 + gate_pre * (1.0 - sig))
    bend = sig * (1.0 - sig) * (2.0 + gate_pre * (1.0 - 2.0 * sig))
    coef[0] = act
    coef[1] = slope
    coef[2] = bend
    up_pre = summed(part, part_in, part_copy, 1) * scale
    hid_ref[0, c] = (coef[0] * up_pre).astype(BF16)
    col_each(lambda a, k: hid_copy(a, k).start(), 0)
    coef[3] = up_pre
    gate_tan = summed(part, part_in, part_copy, 2) * scale
    coef[4] = gate_tan
    up_tan = summed(part, part_in, part_copy, 3) * scale
    hid_ref[1, c] = (coef[1] * coef[4] * coef[3] + coef[0] * up_tan).astype(BF16)
    col_each(lambda a, k: hid_copy(a, k).start(), 1)
    coef[2] = up_tan * coef[1] + coef[3] * coef[2] * coef[4]
    coef[4] = coef[1] * coef[4]
    coef[1] = coef[3] * coef[1]

    def down_product(a, make):
        @pl.loop(0, width // tile_d)
        def _(j):
            cols = pl.ds(pl.multiple_of(j * tile_d, tile_d), tile_d)
            out_part[a, :, :, cols] = make(cols).astype(BF16).reshape(n_group, tokens // n_group, tile_d)

        group_loop(lambda k: out_copy(a, k).start())

    def flat(ref, a):
        value = ref[a]
        return value.reshape(tokens, value.shape[-1])

    loads[4].wait()
    loads[5].wait()
    col_each(lambda a, k: hid_copy(a, k).wait_recv(), 0)
    down_product(0, lambda cols: dot(flat(hid_ref, 0), down[0, :, cols], (1, 0)))
    col_each(lambda a, k: hid_copy(a, k).wait_recv(), 1)
    down_product(
        1,
        lambda cols: dot(flat(hid_ref, 1), down[0, :, cols], (1, 0))
        + dot(flat(hid_ref, 0), down[1, :, cols], (1, 0)),
    )

    def owner_sum(a, start):
        def add(k, value):
            out_copy(a, k).wait_recv()
            return value + out_in[a, lax.rem(g - k + n_group, n_group)].astype(F32)

        return lax.fori_loop(1, n_group, add, start + out_part[a, g].astype(F32))

    outputs = owner_sum(0, x_ref[...].astype(F32))
    err_ref[0, g] = (outputs - t_ref[...].astype(F32)).astype(BF16)
    group_loop(lambda k: err_copy(0, k).start())
    err_ref[1, g] = owner_sum(1, jnp.zeros(x_ref.shape, F32)).astype(BF16)
    group_loop(lambda k: err_copy(1, k).start())

    col_each(lambda k: sc_copy(k).wait_recv())
    scales = scale_all[...].reshape(tokens, 128)[:, :1]
    feats = x_all[...].reshape(tokens, width).astype(F32)
    normed_ref[...] = (feats * scales * gain_ref[...]).astype(BF16).T

    def back_product(a, make):
        @pl.loop(0, hidden // tile_f)
        def _(j):
            rows = pl.ds(pl.multiple_of(j * tile_f, tile_f), tile_f)
            bk_part[a, :, :, rows] = make(rows).astype(BF16).reshape(n_col, tokens // n_col, tile_f)

        col_each(lambda a, k: bk_copy(a, k).start(), a)

    group_loop(lambda k: err_copy(0, k).wait_recv())
    back_product(0, lambda rows: dot(flat(err_ref, 0), down[0, rows, :], (1, 1)))
    group_loop(lambda k: err_copy(1, k).wait_recv())
    back_product(
        1,
        lambda rows: dot(flat(err_ref, 1), down[0, rows, :], (1, 1))
        + dot(flat(err_ref, 0), down[1, rows, :], (1, 1)),
    )

    states[0].wait()
    states[1].wait()

    @pl.loop(0, hidden // TILE)
    def _(i):
        rows = pl.ds(pl.multiple_of(i * TILE, TILE), TILE)
        primal = hid_ref[0, :, :, rows].reshape(tokens, TILE).T
        tangent = hid_ref[1, :, :, rows].reshape(tokens, TILE).T
        for j in range(width // tile_d):
            cols = slice(j * tile_d, (j + 1) * tile_d)
            error = err_ref[0, :, :, cols].reshape(tokens, tile_d)
            error_tan = err_ref[1, :, :, cols].reshape(tokens, tile_d)
            grad = dot(primal, error, (1, 0))
            curve = dot(tangent, error, (1, 0)) + dot(primal, error_tan, (1, 0))
            values = update(new_moment[rows, cols], new_second[rows, cols], down[1, rows, cols], grad, curve)
            new_moment[rows, cols], new_second[rows, cols], step[rows, cols] = values

    back_hidden = summed(bk_part, bk_in, bk_copy, 0)
    back_ref[0, c] = (back_hidden * coef[1]).astype(BF16)
    col_each(lambda a, k: back_copy(a, k).start(), 0)
    back_ref[1, c] = (back_hidden * coef[0]).astype(BF16)
    col_each(lambda a, k: back_copy(a, k).start(), 1)
    back_tan = summed(bk_part, bk_in, bk_copy, 1)
    back_ref[2, c] = (back_tan * coef[1] + back_hidden * coef[2]).astype(BF16)
    col_each(lambda a, k: back_copy(a, k).start(), 2)
    back_ref[3, c] = (back_tan * coef[0] + back_hidden * coef[4]).astype(BF16)
    col_each(lambda a, k: back_copy(a, k).start(), 3)

    for state in states[2:]:
        state.wait()
    for a in range(4):
        col_each(lambda a, k: back_copy(a, k).wait_recv(), a)

    def sent(k):
        x_copy(k).wait_send()
        for a in range(2):
            out_copy(a, k).wait_send()
            err_copy(a, k).wait_send()

    group_loop(sent)
    for k in range(1, n_col):
        sq_copy(k).wait_send()
        sc_copy(k).wait_send()
        for a in range(4):
            part_copy(a, k).wait_send()
            back_copy(a, k).wait_send()
        for a in range(2):
            hid_copy(a, k).wait_send()
            bk_copy(a, k).wait_send()


def run_exchange(mesh, x, t, gain, *large):
    n_row, n_col, n_depth = mesh.shape["row"], mesh.shape["col"], mesh.shape["depth"]
    n_group = n_row * n_depth
    rows, width = x.shape
    hidden = large[0].shape[1]
    tokens = rows * n_group
    run = tokens // n_col
    vmem = pl.BlockSpec(memory_space=pltpu.VMEM)
    hbm = pl.BlockSpec(memory_space=pltpu.HBM)
    sem = pltpu.SemaphoreType.DMA
    pair = lambda *shape: [sem(shape), sem(shape)]
    buffers = [
            pltpu.VMEM((2, n_col, run, hidden), BF16),
            pltpu.VMEM((2, n_group, rows, width), BF16),
            pltpu.VMEM((2, width, hidden), BF16),
            pltpu.VMEM((2, hidden, width), BF16),
            pltpu.VMEM((n_group, rows, width), BF16),
            pltpu.VMEM((tokens, width), BF16),
            pltpu.VMEM((n_col, run, 128), F32),
            pltpu.VMEM((n_col, run, 128), F32),
            pltpu.VMEM((n_col, run, 128), F32),
            pltpu.VMEM((4, n_col, run, hidden), BF16),
            pltpu.VMEM((4, n_col, run, hidden), BF16),
            pltpu.VMEM((5, run, hidden), F32),
            pltpu.VMEM((2, n_group, rows, width), BF16),
            pltpu.VMEM((2, n_group, rows, width), BF16),
            pltpu.VMEM((2, n_col, run, hidden), BF16),
            pltpu.VMEM((2, n_col, run, hidden), BF16),
    ]
    size = sum(math.prod(b.shape) * jnp.dtype(b.dtype).itemsize for b in buffers)
    limit = size + 2**20 + 8 * tokens * width
    held = pl.pallas_call(
        functools.partial(exchange, n_row, n_col, n_depth),
        out_shape=(
            pltpu.VMEM((width, tokens), BF16),
            pltpu.VMEM((4, n_col, run, hidden), BF16),
            pltpu.VMEM((2, width, hidden), BF16),
            pltpu.VMEM((2, width, hidden), F32),
            pltpu.VMEM((2, width, hidden), F32),
            *[pltpu.VMEM((hidden, width), F32)] * 3,
        ),
        in_specs=[vmem] * 3 + [hbm] * len(large),
        out_specs=(vmem,) * 8,
        scratch_shapes=[
            *buffers,
            sem((6,)),
            sem((6,)),
            *pair(n_group), *pair(n_col), *pair(n_col), *pair(4, n_col), *pair(2, n_col),
            *pair(2, n_group), *pair(2, n_group), *pair(2, n_col), *pair(4, n_col),
        ],
        compiler_params=pltpu.CompilerParams(
            collective_id=0, has_side_effects=True, vmem_limit_bytes=limit
        ),
    )(x, t, gain.reshape(1, width), *(pltpu.with_memory_space_constraint(a, pltpu.HBM) for a in large))
    return held, limit


def finish(
    normed, back, probes, moments, seconds, down_moment, down_second, down_step,
    gate_out, up_out, down_out, gate_second, up_second, down_second_out, gate_step, up_step, down_step_out,
    stage, stage_sem, down_sem,
):
    writes = [
        pltpu.make_async_copy(src, dst, down_sem.at[i])
        for i, (src, dst) in enumerate([
            (down_moment, down_out), (down_second, down_second_out), (down_step, down_step_out)
        ])
    ]
    for write in writes:
        write.start()
    width, hidden = gate_out.shape
    tokens = normed.shape[1]
    tiles = width // TILE
    tile_f = min(256, hidden)

    def write_back(which, i, slot):
        rows = pl.ds(pl.multiple_of(i * TILE, TILE), TILE)
        outs = (up_out, up_second, up_step) if which else (gate_out, gate_second, gate_step)
        return [
            pltpu.make_async_copy(stage.at[slot, n], out.at[rows], stage_sem.at[slot, n])
            for n, out in enumerate(outs)
        ]

    for which in range(2):

        @pl.loop(0, tiles)
        def _(i):
            rows = pl.ds(pl.multiple_of(i * TILE, TILE), TILE)
            slot = lax.rem(which * tiles + i, 2)

            def drain():
                for copy in write_back(which, i, slot):
                    copy.wait()

            if which:
                drain()
            else:
                pl.when(i >= 2)(drain)
            left = normed[rows, :]
            for j in range(hidden // tile_f):
                cols = slice(j * tile_f, (j + 1) * tile_f)
                grad = dot(left, back[which, :, :, cols].reshape(tokens, tile_f), (1, 0))
                curve = dot(left, back[which + 2, :, :, cols].reshape(tokens, tile_f), (1, 0))
                values = update(
                    moments[which, rows, cols], seconds[which, rows, cols], probes[which, rows, cols], grad, curve
                )
                for n, value in enumerate(values):
                    stage[slot, n, :, cols] = value
            for copy in write_back(which, i, slot):
                copy.start()

    for i in (tiles - 2, tiles - 1):
        for copy in write_back(1, i, (tiles + i) % 2):
            copy.wait()
    for write in writes:
        write.wait()


def run_finish(held, front, down, limit):
    hidden = front[1]
    vmem = pl.BlockSpec(memory_space=pltpu.VMEM)
    hbm = pl.BlockSpec(memory_space=pltpu.HBM)
    shapes = [jax.ShapeDtypeStruct(size, F32) for size in (front, front, down)]
    return pl.pallas_call(
        finish,
        out_shape=tuple(shapes) * 3,
        in_specs=[vmem] * len(held),
        out_specs=(hbm,) * 9,
        scratch_shapes=[
            pltpu.VMEM((2, 3, TILE, hidden), F32),
            pltpu.SemaphoreType.DMA((2, 3)),
            pltpu.SemaphoreType.DMA((3,)),
        ],
        compiler_params=pltpu.CompilerParams(vmem_limit_bytes=limit),
    )(*(pltpu.with_memory_space_constraint(a, pltpu.VMEM) for a in held))


def shards(
    mesh, inputs, targets, norm_gain, w_gate, w_up, w_down, probe_gate, probe_up, probe_down,
    moment_gate, moment_up, moment_down, second_gate, second_up, second_down,
):
    held, limit = run_exchange(
        mesh, inputs, targets, norm_gain, w_gate, w_up, w_down, probe_gate, probe_up, probe_down,
        moment_gate, moment_up, moment_down, second_gate, second_up, second_down,
    )
    return run_finish(held, moment_gate.shape, moment_down.shape, limit)


def solution(mesh):
    group = ("row", "depth")
    rows, cols = P(group, "col"), P("col", group)
    return jax.shard_map(
        functools.partial(shards, mesh),
        mesh=mesh,
        in_specs=(rows, rows, P("col"), cols, cols, rows) + (cols, cols, rows) * 3,
        out_specs=(cols, cols, rows) * 3,
        check_vma=False,
    )
```
